32 devices in a mesh: dp: 4 (over z), expert: 8 (over y, x, core).
Axes of the slice: x: 2, y: 2, z: 4, core: 2. Of those that a mesh axis runs over, the one named last changes fastest.
Arguments:
- tokens: bfloat16 [6304, 768], P(('dp', 'expert')), may hold values from -6 to 6
- cotangent: bfloat16 [6304, 768], P(('dp', 'expert')), may hold values from -6 to 6
- routes: int32 [6304, 2], P(('dp', 'expert')), may hold values from 0 to 7, all different within a row; in each aligned block of 197 rows (0 to 196, 197 to 393, ...) at most 50 rows name the same one
- priority: int32 [32, 197], P(('dp', 'expert')), may hold values from 0 to 196, each once within a row
- ln_gains: float32 [2, 768], replicated, may hold values from 0.5 to 1.5
- ln_biases: float32 [2, 768], replicated, may hold values from -2 to 2
- qkv_weight: bfloat16 [768, 2304], P('expert'), may hold values from -0.21875 to 0.21875
- out_weight: bfloat16 [768, 768], P('expert'), may hold values from -1.25 to 1.25
- router: float32 [768, 8], replicated, may hold values from -0.21875 to 0.21875
- w_in: bfloat16 [8, 768, 1536], P('expert'), may hold values from -0.21875 to 0.21875
- w_out: bfloat16 [8, 768, 1536], P('expert'), may hold values from -0.21875 to 0.21875
- norm_momentum: float32 [4, 768], replicated, may hold values from -128 to 128
- router_momentum: float32 [768, 8], replicated, may hold values from -6000 to 6000
- qkv_momentum: float32 [768, 2304], P('expert'), may hold values from -1200 to 1200
- out_momentum: float32 [768, 768], P('expert'), may hold values from -600 to 600
- w_in_momentum: float32 [8, 768, 1536], P('expert', 'dp'), may hold values from -180 to 180
- w_out_momentum: float32 [8, 768, 1536], P('expert', 'dp'), may hold values from -180 to 180
Outputs:
- block_out: float32 [6304, 768], P(('dp', 'expert'))
- grad_tokens: float32 [6304, 768], P(('dp', 'expert'))
- grad_norm: float32 [4, 768], replicated
- grad_router: float32 [768, 8], replicated
- grad_qkv: float32 [768, 2304], P('expert')
- grad_out: float32 [768, 768], P('expert')
- grad_w_in: float32 [8, 768, 1536], P('expert', 'dp')
- grad_w_out: float32 [8, 768, 1536], P('expert', 'dp')
- new_norm: float32 [4, 768], replicated
- new_norm_momentum: float32 [4, 768], replicated
- new_router: float32 [768, 8], replicated
- new_router_momentum: float32 [768, 8], replicated
- new_qkv: float32 [768, 2304], P('expert')
- new_qkv_momentum: float32 [768, 2304], P('expert')
- new_out: float32 [768, 768], P('expert')
- new_out_momentum: float32 [768, 768], P('expert')
- new_w_in: float32 [8, 768, 1536], P('expert', 'dp')
- new_w_in_momentum: float32 [8, 768, 1536], P('expert', 'dp')
- new_w_out: float32 [8, 768, 1536], P('expert', 'dp')
- new_w_out_momentum: float32 [8, 768, 1536], P('expert', 'dp')
The draws below stay inside these ranges and needn't reach their ends.
Inputs may be any that keep to these rules, and one draw needn't show every extreme that they name: `routes`: each row names two different experts. In the rows of one device no expert is named more than 2 * 25 times. `priority`: each row is an ordering of the 197 tokens of one block.
All inputs are finite; a program needn't handle non-finite values.
Results may differ from the reference program's by a relative error of at most 0.011.
Values may be sent and summed in bfloat16 or wider, within the bound.
A program may use at most 128 MiB of HBM per device.

```python
import math
import jax
import jax.numpy as jnp
import numpy as np
from jax import lax

D = 768
HEADS = 12
FF = 1536
NS_STEPS = 5
SEQ = 197
TOK_DEV = 197
EXPERTS = 8
TOKENS = 6304
CAPACITY = 25
N_DP = 4
N_EXPERT = 8


def scaled_values(key, leading, row_count, col_count, spread):
    subkeys = jax.random.split(key, 3)
    rising = jnp.exp(jnp.log(3.0) * jnp.arange(row_count, dtype=jnp.float32) / row_count)
    row_scale = rising[None, :, None] * jnp.exp(jax.random.uniform(subkeys[0], (leading, row_count, 1), minval=0.0, maxval=1.3862944))
    col_scale = jnp.exp(jax.random.uniform(subkeys[1], (leading, 1, col_count), minval=0.0, maxval=2.3025851))
    values = jnp.clip(jax.random.normal(subkeys[2], (leading, row_count, col_count)), -4.0, 4.0)
    return spread * 0.125 * row_scale * col_scale * values


def draw_router_momentum(key, part):
    return scaled_values(jax.random.fold_in(key, 11), 1, D, EXPERTS, 100.0)[0]


def draw_qkv_momentum(key, part):
    return scaled_values(jax.random.fold_in(key, 14), 1, D, 3 * D, 20.0)[0]


def draw_out_momentum(key, part):
    return scaled_values(jax.random.fold_in(key, 15), 1, D, D, 10.0)[0]


def draw_w_in_momentum(key, part):
    return scaled_values(jax.random.fold_in(key, 12), EXPERTS, D, FF, 3.0)


def draw_w_out_momentum(key, part):
    return scaled_values(jax.random.fold_in(key, 13), EXPERTS, D, FF, 3.0)


def levels(stream_key, shape, shards, smallest, largest):
    level, own = 1.0, jax.random.fold_in(stream_key, 6)
    for position, blocks in shards:
        heights = jnp.exp(jax.random.uniform(jax.random.fold_in(own, position), (blocks,), jnp.float32, smallest / len(shards), largest / len(shards)))
        level = level * jnp.repeat(heights, shape[position] // blocks).reshape([-1 if axis == position else 1 for axis in range(len(shape))])
    return level


def assign_block(key, own, number, rows, amount, top, limit, slope):
    order = jax.random.permutation(key, amount)
    crowded, ordinary = portions_of(amount, rows * top, limit, slope, True), portions_of(amount, rows * top, limit, slope, False)
    places = jnp.arange(amount)

    def named(tallies, turn):
        used = int((tallies > 0).sum())
        fixed = max(1, used // 4)
        moved = fixed + (places - fixed + turn * (used - fixed)) % max(1, amount - fixed)
        return jnp.zeros((amount,), jnp.int32).at[order[jnp.where(places < fixed, places, moved)]].set(jnp.asarray(tallies, jnp.int32))

    tallies = jnp.where(number % 4 == 0, named(crowded, number // 4), named(ordinary, number - number // 4 - 1))
    mixed = jax.random.permutation(jax.random.fold_in(own, 3), amount)
    donor, receiver = mixed[0:amount // 2 * 2:2], mixed[1:amount // 2 * 2:2]
    room = jnp.minimum(tallies[donor] - 1, limit - tallies[receiver]) // 2
    room = jnp.where((donor == order[0]) | (receiver == order[0]) | (tallies[receiver] == 0), 0, jnp.maximum(room, 0))
    moved = jax.random.randint(jax.random.fold_in(own, 4), (amount // 2,), 0, 1 << 20) % (room + 1)
    tallies = tallies.at[donor].add(-moved).at[receiver].add(moved)
    items = jnp.searchsorted(jnp.cumsum(tallies), jnp.arange(rows * top), side="right").astype(jnp.int32)
    grid = items.reshape(top, rows).T
    grid = grid[jax.random.permutation(jax.random.fold_in(own, 1), rows)]
    turn = jax.random.randint(jax.random.fold_in(own, 2), (rows, 1), 0, top)
    return jnp.take_along_axis(grid, (jnp.arange(top)[None, :] + turn) % top, axis=1)


def portions_of(count, total, bound, skew, full):
    loads = [(1 << 20) // math.isqrt(grade ** skew) + 1 for grade in range(1, count + 1)]
    largest = bound if full else min(bound, max(-(-total // count), total * loads[0] // sum(loads)))
    least = 1 if total - largest >= count - 1 else 0
    holding, rest = [largest] + [least] * (count - 1), total - largest - least * (count - 1)
    while rest > 0:
        candidates = [i for i in range(1, count) if holding[i] < largest] or [i for i in range(1, count) if holding[i] < bound]
        whole, remaining = sum([loads[i] for i in candidates]), rest
        for i in candidates:
            addition = min(bound - holding[i], max(1, remaining * loads[i] // whole), rest)
            holding[i] = holding[i] + addition
            rest = rest - addition
    return np.array(holding)


def noise(own_key, dims, scale, bound, cuts=(), kind=jnp.bfloat16):
    drawn = jax.random.normal(own_key, dims, jnp.float32) * scale
    if len(cuts) > 0:
        drawn = levels(own_key, dims, cuts, -0.22, 0.18) * drawn
    return jnp.clip(drawn, min=-bound, max=bound).astype(kind)


def setup_inputs(seed: int = 0) -> dict:
    splits = jax.random.split(jax.random.key(seed), 18)
    tokens = noise(splits[0], (TOKENS, D), 1.0, 6.0, ((0, 32),))
    cotangent = noise(splits[1], (TOKENS, D), 1.0, 6.0, ((0, 32),))
    routes_keys = jax.random.split(jax.random.fold_in(splits[2], 1), TOKENS // TOK_DEV)
    routes_turns = jax.random.permutation(jax.random.fold_in(splits[2], 3), TOKENS // TOK_DEV)
    routes = jax.vmap(lambda own, number: assign_block(jax.random.fold_in(splits[2], 2), own, number, TOK_DEV, EXPERTS, 2, 2 * CAPACITY, 2))(routes_keys, routes_turns).reshape((TOKENS, 2))
    priority = jax.vmap(lambda own: jax.random.permutation(own, TOK_DEV))(jax.random.split(splits[3], (N_DP * N_EXPERT))).reshape((N_DP * N_EXPERT, TOK_DEV)).astype(jnp.int32)
    ln_gains = jnp.clip(1.0 + 0.1 * jax.random.normal(splits[4], (2, D), jnp.float32), 0.5, 1.5)
    ln_biases = noise(splits[5], (2, D), 0.3, 2.0, (), jnp.float32)
    qkv_weight = noise(splits[6], (D, 3 * D), D ** -0.5, 0.21875, ((0, 8),))
    out_weight = noise(splits[7], (D, D), (D // 32) ** -0.5, 1.25, ((0, 8),))
    router = noise(splits[8], (D, EXPERTS), D ** -0.5, 0.21875, (), jnp.float32)
    w_in = noise(splits[9], (EXPERTS, D, FF), D ** -0.5, 0.21875, ((0, 8),))
    w_out = noise(splits[10], (EXPERTS, D, FF), (FF // 2) ** -0.5, 0.21875, ((0, 8),))
    norm_momentum = noise(splits[11], (4, D), 20.0, 128.0, (), jnp.float32)
    router_momentum = draw_router_momentum(jax.random.fold_in(splits[17], 71), 0)
    qkv_momentum = draw_qkv_momentum(jax.random.fold_in(splits[17], 71), 0)
    out_momentum = draw_out_momentum(jax.random.fold_in(splits[17], 71), 0)
    w_in_momentum = draw_w_in_momentum(jax.random.fold_in(splits[17], 71), 0)
    w_out_momentum = draw_w_out_momentum(jax.random.fold_in(splits[17], 71), 0)
    return dict(tokens=tokens, cotangent=cotangent, routes=routes, priority=priority, ln_gains=ln_gains, ln_biases=ln_biases, qkv_weight=qkv_weight, out_weight=out_weight, router=router, w_in=w_in, w_out=w_out, norm_momentum=norm_momentum, router_momentum=router_momentum, qkv_momentum=qkv_momentum, out_momentum=out_momentum, w_in_momentum=w_in_momentum, w_out_momentum=w_out_momentum)


quintic_one = 3.4445
quintic_two = -4.775
quintic_three = 2.0315
decay_rate = 0.9
matrix_rate = 0.2
norm_rate = 0.004
norm_eps = 1e-06
frob_eps = 1e-07
highest = lax.Precision.HIGHEST
contract_last = (((1,), (1,)), ((), ()))
contract_first = (((0,), (0,)), ((), ()))

def rounded(values):
    return lax.optimization_barrier(values.astype(jnp.bfloat16)).astype(jnp.float32)

def gelu_slope(preact):
    return 0.5 * (1.0 + lax.erf(preact * 0.7071067811865476)) + preact * jnp.exp(-0.5 * preact * preact) * 0.3989422804014327

def layer_stats(token_rows, gain, bias):
    centre = token_rows - lax.optimization_barrier(jnp.mean(token_rows, axis=-1, keepdims=True))
    inverse = lax.rsqrt(lax.optimization_barrier(jnp.mean(centre * centre, axis=-1, keepdims=True)) + norm_eps)
    scaled = centre * inverse
    return (scaled, inverse, scaled * gain + bias)

def slot_index(choice_ids, order_rows, experts, capacity):
    token_count = choice_ids.shape[0]
    ranked = jnp.take(choice_ids, order_rows, axis=0)
    entries = jnp.concatenate([ranked[:, 0], ranked[:, 1]])
    onehot = (entries[:, None] == jnp.arange(experts, dtype=jnp.int32)[None, :]).astype(jnp.int32)
    before = jnp.cumsum(onehot, axis=0) - onehot
    ranked_slots = lax.optimization_barrier(jnp.sum(before * onehot, axis=1)).reshape(2, token_count).T
    slot_values = jnp.zeros((token_count, 2), jnp.int32).at[order_rows].set(ranked_slots)
    return jnp.where(slot_values < capacity, choice_ids * capacity + slot_values, experts * capacity).astype(jnp.int32)

def gates_of(logits, choice_ids):
    chosen = jnp.take_along_axis(logits, choice_ids, axis=1)
    first_gate = jax.nn.sigmoid(chosen[:, 0] - chosen[:, 1])
    return jnp.stack([first_gate, 1.0 - first_gate], axis=1)

def input_grad(base_grad, normed_grad, scaled, inverse, gain):
    lifted = normed_grad * gain
    centred = lifted - lax.optimization_barrier(jnp.mean(lifted, axis=-1, keepdims=True)) - scaled * lax.optimization_barrier(jnp.mean(lifted * scaled, axis=-1, keepdims=True))
    return base_grad + inverse * centred

def ortho_wide(matrix):
    iterate = (matrix / (jnp.sqrt(jnp.sum(matrix * matrix)) + frob_eps)).astype(jnp.bfloat16)
    for iteration in range(NS_STEPS):
        gram_matrix = lax.dot_general(iterate, iterate, contract_last, preferred_element_type=jnp.float32).astype(jnp.bfloat16)
        mixer_matrix = (quintic_two * gram_matrix.astype(jnp.float32) + quintic_three * jnp.dot(gram_matrix, gram_matrix, preferred_element_type=jnp.float32)).astype(jnp.bfloat16)
        iterate = (quintic_one * iterate.astype(jnp.float32) + jnp.dot(mixer_matrix, iterate, preferred_element_type=jnp.float32)).astype(jnp.bfloat16)
    return iterate

def ortho_tall(matrix):
    iterate = (matrix / (jnp.sqrt(jnp.sum(matrix * matrix)) + frob_eps)).astype(jnp.bfloat16)
    for iteration in range(NS_STEPS):
        gram_matrix = lax.dot_general(iterate, iterate, contract_first, preferred_element_type=jnp.float32).astype(jnp.bfloat16)
        mixer_matrix = (quintic_two * gram_matrix.astype(jnp.float32) + quintic_three * jnp.dot(gram_matrix, gram_matrix, preferred_element_type=jnp.float32)).astype(jnp.bfloat16)
        iterate = (quintic_one * iterate.astype(jnp.float32) + jnp.dot(iterate, mixer_matrix, preferred_element_type=jnp.float32)).astype(jnp.bfloat16)
    return iterate

def split_heads(qkv_rows):
    shaped = qkv_rows.astype(jnp.float32).reshape(-1, SEQ, 3, HEADS, D // HEADS)
    return (shaped[:, :, 0], shaped[:, :, 1], shaped[:, :, 2])

def attend_forward(qkv_rows):
    query_rows, key_rows, value_rows = split_heads(qkv_rows)
    score_scale = 1.0 / math.sqrt(D // HEADS)
    scores = jnp.einsum('ishd,ithd->ihst', query_rows, key_rows) * score_scale
    log_total = jnp.log(lax.optimization_barrier(jnp.sum(jnp.exp(scores), axis=3, keepdims=True)))
    attn_probs = rounded(jnp.exp(scores - log_total))
    mixed_rows = jnp.einsum('ihst,ithd->ishd', attn_probs, value_rows).astype(jnp.bfloat16).reshape(-1, D)
    return (mixed_rows, log_total)

def attend_backward(qkv_rows, log_total, mixed_grad):
    query_rows, key_rows, value_rows = split_heads(qkv_rows)
    score_scale = 1.0 / math.sqrt(D // HEADS)
    scores = jnp.einsum('ishd,ithd->ihst', query_rows, key_rows) * score_scale
    attn_probs = rounded(jnp.exp(scores - log_total))
    grad_heads = mixed_grad.astype(jnp.float32).reshape(-1, SEQ, HEADS, D // HEADS)
    value_grad = jnp.einsum('ihst,ishd->ithd', attn_probs, grad_heads)
    prob_grad = jnp.einsum('ishd,ithd->ihst', grad_heads, value_rows)
    row_delta = lax.optimization_barrier(jnp.sum(attn_probs * prob_grad, axis=3, keepdims=True))
    score_grad = rounded(attn_probs * (prob_grad - row_delta) * score_scale)
    query_grad = jnp.einsum('ihst,ithd->ishd', score_grad, key_rows)
    key_grad = jnp.einsum('ihst,ishd->ithd', score_grad, query_rows)
    return jnp.stack([query_grad, key_grad, value_grad], axis=2).astype(jnp.bfloat16).reshape(-1, 3 * D)

def reference(tokens, cotangent, routes, priority, ln_gains, ln_biases, qkv_weight, out_weight, router, w_in, w_out, norm_momentum, router_momentum, qkv_momentum, out_momentum, w_in_momentum, w_out_momentum):
    members = EXPERTS
    groups = TOKENS // (TOK_DEV * EXPERTS)
    slots_all = EXPERTS * CAPACITY
    first_weight = w_in.astype(jnp.float32)
    second_weight = w_out.astype(jnp.float32)

    def dispatch_part(middle_rows, choice_ids, order_rows):
        slot_flat = slot_index(choice_ids, order_rows, EXPERTS, CAPACITY)
        scaled, inverse, normed = layer_stats(middle_rows, ln_gains[1], ln_biases[1])
        logits = jnp.dot(normed, router, precision=highest)
        gate_values = gates_of(logits, choice_ids)
        dispatch = jnp.zeros((slots_all, D), jnp.bfloat16).at[slot_flat.reshape(-1)].set(jnp.repeat(normed.astype(jnp.bfloat16), 2, axis=0), mode='drop')
        return (slot_flat, scaled, inverse, normed, gate_values, dispatch)

    def to_experts(buffers):
        return buffers.reshape(members, EXPERTS, CAPACITY, -1).transpose(1, 0, 2, 3).reshape(EXPERTS, members * CAPACITY, -1)

    def from_experts(expert_rows):
        return expert_rows.reshape(EXPERTS, members, CAPACITY, -1).transpose(1, 0, 2, 3).reshape(members, slots_all, -1)

    def combine_part(middle_rows, cot_rows, choice_ids, slot_flat, gate_values, back_rows):
        picked = jnp.take(back_rows, slot_flat.reshape(-1), axis=0, mode='fill', fill_value=0).reshape(TOK_DEV, 2, D).astype(jnp.float32)
        cot_float = cot_rows.astype(jnp.float32)
        block_rows = middle_rows + lax.optimization_barrier(jnp.sum(gate_values[:, :, None] * picked, axis=1))
        gate_grad = lax.optimization_barrier(jnp.sum(picked * cot_float[:, None, :], axis=2))
        logit_step = gate_values[:, 0] * gate_values[:, 1] * (gate_grad[:, 0] - gate_grad[:, 1])
        columns = jnp.arange(EXPERTS, dtype=jnp.int32)[None, :]
        logit_grad = ((choice_ids[:, 0:1] == columns).astype(jnp.float32) - (choice_ids[:, 1:2] == columns).astype(jnp.float32)) * logit_step[:, None]
        weighted = (gate_values[:, :, None] * cot_float[:, None, :]).reshape(-1, D)
        sent_grad = jnp.zeros((slots_all, D), jnp.float32).at[slot_flat.reshape(-1)].set(weighted, mode='drop').astype(jnp.bfloat16)
        return (block_rows, logit_grad, sent_grad)

    def finish_part(cot_rows, slot_flat, scaled, inverse, normed, logit_grad, back_grad):
        gathered = jnp.take(back_grad, slot_flat.reshape(-1), axis=0, mode='fill', fill_value=0).reshape(TOK_DEV, 2, D).astype(jnp.float32)
        normed_grad = lax.optimization_barrier(jnp.sum(gathered, axis=1)) + lax.dot_general(logit_grad, router, contract_last, precision=highest)
        router_local = lax.dot_general(normed, logit_grad, contract_first, precision=highest)
        norm_local = jnp.stack([lax.optimization_barrier(jnp.sum(normed_grad * scaled, axis=0)), lax.optimization_barrier(jnp.sum(normed_grad, axis=0))])
        middle_grad = input_grad(cot_rows.astype(jnp.float32), normed_grad, scaled, inverse, ln_gains[1])
        return (middle_grad, router_local, norm_local)

    def group_step(running, inputs):
        token_rows, cot_rows, choice_ids, order_rows = inputs
        flat_tokens = token_rows.reshape(members * TOK_DEV, D).astype(jnp.float32)
        scaled_one, inverse_one, normed_one = layer_stats(flat_tokens, ln_gains[0], ln_biases[0])
        attn_in = normed_one.astype(jnp.bfloat16)
        qkv_rows = jnp.dot(attn_in, qkv_weight, preferred_element_type=jnp.float32).astype(jnp.bfloat16)
        mixed_rows, log_total = attend_forward(qkv_rows)
        middle_rows = flat_tokens + jnp.dot(mixed_rows, out_weight, preferred_element_type=jnp.float32)
        member_rows = middle_rows.reshape(members, TOK_DEV, D)
        slot_flat, scaled, inverse, normed, gate_values, dispatch = jax.vmap(dispatch_part)(member_rows, choice_ids, order_rows)
        expert_rows = to_experts(dispatch)
        preact = jnp.einsum('erd,edf->erf', expert_rows.astype(jnp.float32), first_weight)
        active = jax.nn.gelu(preact, approximate=False).astype(jnp.bfloat16)
        result = jnp.einsum('erf,edf->erd', active.astype(jnp.float32), second_weight).astype(jnp.bfloat16)
        block_rows, logit_grad, sent_grad = jax.vmap(combine_part)(member_rows, cot_rows, choice_ids, slot_flat, gate_values, from_experts(result))
        grad_rows = to_experts(sent_grad)
        act_grad = jnp.einsum('erd,edf->erf', grad_rows.astype(jnp.float32), second_weight)
        pre_grad = (act_grad * gelu_slope(preact)).astype(jnp.bfloat16)
        row_grad = jnp.einsum('erf,edf->erd', pre_grad.astype(jnp.float32), first_weight).astype(jnp.bfloat16)
        first_grad = jnp.einsum('erd,erf->edf', expert_rows.astype(jnp.float32), pre_grad.astype(jnp.float32))
        second_grad = jnp.einsum('erd,erf->edf', grad_rows.astype(jnp.float32), active.astype(jnp.float32))
        middle_grad, router_local, norm_local = jax.vmap(finish_part)(cot_rows, slot_flat, scaled, inverse, normed, logit_grad, from_experts(row_grad))
        middle_flat = middle_grad.reshape(members * TOK_DEV, D)
        middle_rounded = middle_flat.astype(jnp.bfloat16)
        mixed_grad = lax.dot_general(middle_rounded, out_weight, contract_last, preferred_element_type=jnp.float32).astype(jnp.bfloat16)
        qkv_grad = attend_backward(qkv_rows, log_total, mixed_grad)
        attn_in_grad = lax.dot_general(qkv_grad, qkv_weight, contract_last, preferred_element_type=jnp.float32)
        tokens_grad = input_grad(middle_flat, attn_in_grad, scaled_one, inverse_one, ln_gains[0])
        qkv_term = lax.dot_general(attn_in, qkv_grad, contract_first, preferred_element_type=jnp.float32)
        out_term = lax.dot_general(mixed_rows, middle_rounded, contract_first, preferred_element_type=jnp.float32)
        second_norm = lax.optimization_barrier(jnp.sum(norm_local, axis=0))
        norm_rows = jnp.stack([lax.optimization_barrier(jnp.sum(attn_in_grad * scaled_one, axis=0)), second_norm[0], lax.optimization_barrier(jnp.sum(attn_in_grad, axis=0)), second_norm[1]])
        total_first, total_second, total_router, total_norm, total_qkv, total_out = running
        running = (total_first + first_grad, total_second + second_grad, total_router + lax.optimization_barrier(jnp.sum(router_local, axis=0)), total_norm + norm_rows, total_qkv + qkv_term, total_out + out_term)
        return (running, (block_rows.reshape(members * TOK_DEV, D), tokens_grad))
    initial = (jnp.zeros((EXPERTS, D, FF), jnp.float32), jnp.zeros((EXPERTS, D, FF), jnp.float32), jnp.zeros((D, EXPERTS), jnp.float32), jnp.zeros((4, D), jnp.float32), jnp.zeros((D, 3 * D), jnp.float32), jnp.zeros((D, D), jnp.float32))
    inputs = (tokens.reshape(groups, members, TOK_DEV, D), cotangent.reshape(groups, members, TOK_DEV, D), routes.reshape(groups, members, TOK_DEV, 2), priority.reshape(groups, members, TOK_DEV))
    totals, stacked = lax.scan(group_step, initial, inputs)
    grad_w_in, grad_w_out, grad_router, grad_norm, grad_qkv, grad_out = totals
    block_out = stacked[0].reshape(TOKENS, D)
    grad_tokens = stacked[1].reshape(TOKENS, D)
    new_norm_momentum = decay_rate * norm_momentum + grad_norm
    new_norm = jnp.concatenate([ln_gains, ln_biases], axis=0) - norm_rate * new_norm_momentum
    new_router_momentum = decay_rate * router_momentum + grad_router
    new_router = router - matrix_rate * ortho_tall(new_router_momentum).astype(jnp.float32)
    new_qkv_momentum = decay_rate * qkv_momentum + grad_qkv
    new_qkv = qkv_weight.astype(jnp.float32) - matrix_rate * math.sqrt(3.0) * ortho_wide(new_qkv_momentum).astype(jnp.float32)
    new_out_momentum = decay_rate * out_momentum + grad_out
    new_out = out_weight.astype(jnp.float32) - matrix_rate * ortho_wide(new_out_momentum).astype(jnp.float32)
    widen_factor = math.sqrt(max(1.0, FF / D))

    def expert_update(members_tuple):
        first_weight_e, first_moment, first_grad, second_weight_e, second_moment, second_grad = members_tuple
        first_new_moment = decay_rate * first_moment + first_grad
        second_new_moment = decay_rate * second_moment + second_grad
        first_new = first_weight_e.astype(jnp.float32) - matrix_rate * widen_factor * ortho_wide(first_new_moment).astype(jnp.float32)
        second_new = second_weight_e.astype(jnp.float32) - matrix_rate * ortho_wide(second_new_moment).astype(jnp.float32)
        return (first_new, first_new_moment, second_new, second_new_moment)
    new_w_in, new_w_in_momentum, new_w_out, new_w_out_momentum = lax.map(expert_update, (w_in, w_in_momentum, grad_w_in, w_out, w_out_momentum, grad_w_out))
    return (block_out, grad_tokens, grad_norm, grad_router, grad_qkv, grad_out, grad_w_in, grad_w_out, new_norm, new_norm_momentum, new_router, new_router_momentum, new_qkv, new_qkv_momentum, new_out, new_out_momentum, new_w_in, new_w_in_momentum, new_w_out, new_w_out_momentum)
```

```python
import math

import jax
import jax.numpy as jnp
from jax import lax
from jax.sharding import PartitionSpec as P

HEADS = 12
NS_STEPS = 5
SEQ = 197


quintic_one = 3.4445
quintic_two = -4.775
quintic_three = 2.0315
decay_rate = 0.9
matrix_rate = 0.2
norm_rate = 0.004
norm_eps = 1e-06
frob_eps = 1e-07
highest = lax.Precision.HIGHEST
contract_last = (((1,), (1,)), ((), ()))
contract_first = (((0,), (0,)), ((), ()))


def gelu_slope(preact):
    return (
        0.5 * (1.0 + lax.erf(preact * 0.7071067811865476))
        + preact * jnp.exp(-0.5 * preact * preact) * 0.3989422804014327
    )


def layer_stats(token_rows, gain, bias):
    centre = token_rows - jnp.mean(token_rows, axis=-1, keepdims=True)
    inverse = lax.rsqrt(jnp.mean(centre * centre, axis=-1, keepdims=True) + norm_eps)
    scaled = centre * inverse
    return (scaled, inverse, scaled * gain + bias)


def slot_index(choice_ids, order_rows, experts, capacity):
    token_count = choice_ids.shape[0]
    ranked = jnp.take(choice_ids, order_rows, axis=0)
    entries = jnp.concatenate([ranked[:, 0], ranked[:, 1]])
    onehot = (entries[:, None] == jnp.arange(experts, dtype=jnp.int32)[None, :]).astype(jnp.int32)
    before = jnp.cumsum(onehot, axis=0) - onehot
    ranked_slots = jnp.sum(before * onehot, axis=1).reshape(2, token_count).T
    slot_values = jnp.zeros((token_count, 2), jnp.int32).at[order_rows].set(ranked_slots)
    return jnp.where(
        slot_values < capacity, choice_ids * capacity + slot_values, experts * capacity
    )


def gates_of(logits, choice_ids):
    chosen = jnp.take_along_axis(logits, choice_ids, axis=1)
    first_gate = jax.nn.sigmoid(chosen[:, 0] - chosen[:, 1])
    return jnp.stack([first_gate, 1.0 - first_gate], axis=1)


def input_grad(base_grad, normed_grad, scaled, inverse, gain):
    lifted = normed_grad * gain
    centred = (
        lifted
        - jnp.mean(lifted, axis=-1, keepdims=True)
        - scaled * jnp.mean(lifted * scaled, axis=-1, keepdims=True)
    )
    return base_grad + inverse * centred


def ortho_tall(matrix):
    iterate = (matrix / (jnp.sqrt(jnp.sum(matrix * matrix)) + frob_eps)).astype(jnp.bfloat16)
    for iteration in range(NS_STEPS):
        gram_matrix = lax.dot_general(
            iterate, iterate, contract_first, preferred_element_type=jnp.float32
        ).astype(jnp.bfloat16)
        mixer_matrix = (
            quintic_two * gram_matrix.astype(jnp.float32)
            + quintic_three * jnp.dot(gram_matrix, gram_matrix, preferred_element_type=jnp.float32)
        ).astype(jnp.bfloat16)
        iterate = (
            quintic_one * iterate.astype(jnp.float32)
            + jnp.dot(iterate, mixer_matrix, preferred_element_type=jnp.float32)
        ).astype(jnp.bfloat16)
    return iterate


def ortho_rows(moment, row_start, row_count):
    norm = jnp.sqrt(jnp.sum(moment * moment)) + frob_eps
    iterate = (moment / norm).astype(jnp.bfloat16)
    for iteration in range(NS_STEPS):
        gram = lax.dot_general(
            iterate, iterate, contract_last, preferred_element_type=jnp.float32
        ).astype(jnp.bfloat16)
        gram_part, iter_part = gram, iterate
        if iteration == NS_STEPS - 1:
            gram_part = lax.dynamic_slice_in_dim(gram, row_start, row_count, 0)
            iter_part = lax.dynamic_slice_in_dim(iterate, row_start, row_count, 0)
        mixer = (
            quintic_two * gram_part.astype(jnp.float32)
            + quintic_three * jnp.dot(gram_part, gram, preferred_element_type=jnp.float32)
        ).astype(jnp.bfloat16)
        iterate = (
            quintic_one * iter_part.astype(jnp.float32)
            + jnp.dot(mixer, iterate, preferred_element_type=jnp.float32)
        ).astype(jnp.bfloat16)
    return iterate


def split_heads(qkv_rows, image_count, head_width):
    shaped = qkv_rows.reshape(image_count, SEQ, 3, HEADS, head_width)
    return (shaped[:, :, 0], shaped[:, :, 1], shaped[:, :, 2])


def attention_scores(query_rows, key_rows, score_scale):
    return (
        jnp.einsum("ishd,ithd->ihst", query_rows, key_rows, preferred_element_type=jnp.float32)
        * score_scale
    )


def body(
    tokens,
    cotangent,
    routes,
    priority,
    ln_gains,
    ln_biases,
    qkv_weight,
    out_weight,
    router,
    w_in,
    w_out,
    norm_momentum,
    router_momentum,
    qkv_momentum,
    out_momentum,
    w_in_momentum,
    w_out_momentum,
):
    token_count, model_width = tokens.shape
    experts = router.shape[1]
    hidden_units = w_in.shape[2]
    capacity = (token_count + experts - 1) // experts
    slots_all = experts * capacity
    dp_share = model_width // lax.axis_size("dp")
    image_count = token_count // SEQ
    head_width = model_width // HEADS
    score_scale = 1.0 / math.sqrt(head_width)
    first_weight = w_in[0]
    second_weight = w_out[0]
    cot_float = cotangent.astype(jnp.float32)
    full_qkv, full_out = (
        lax.all_gather(qkv_weight, "expert", axis=0, tiled=True),
        lax.all_gather(out_weight, "expert", axis=0, tiled=True),
    )
    moment_pair = jnp.concatenate(
        [w_in_momentum[0].astype(jnp.bfloat16), w_out_momentum[0].astype(jnp.bfloat16)], axis=1
    )
    token_float = tokens.astype(jnp.float32)
    scaled_one, inverse_one, normed_one = layer_stats(token_float, ln_gains[0], ln_biases[0])
    attn_in = normed_one.astype(jnp.bfloat16)
    qkv_rows = jnp.dot(attn_in, full_qkv, preferred_element_type=jnp.float32).astype(jnp.bfloat16)
    query_rows, key_rows, value_rows = split_heads(qkv_rows, image_count, head_width)
    scores = attention_scores(query_rows, key_rows, score_scale)
    log_total = jnp.log(jnp.sum(jnp.exp(scores), axis=3, keepdims=True))
    attn_probs = jnp.exp(scores - log_total).astype(jnp.bfloat16)
    mixed_rows = (
        jnp.einsum("ihst,ithd->ishd", attn_probs, value_rows, preferred_element_type=jnp.float32)
        .astype(jnp.bfloat16)
        .reshape(token_count, model_width)
    )
    middle_rows = token_float + jnp.dot(mixed_rows, full_out, preferred_element_type=jnp.float32)
    slot_flat = slot_index(routes, priority[0], experts, capacity)
    scaled, inverse, normed = layer_stats(middle_rows, ln_gains[1], ln_biases[1])
    logits = jnp.dot(normed, router, precision=highest)
    gate_values = gates_of(logits, routes)
    position = jnp.arange(slots_all, dtype=jnp.int32)[:, None]
    pick_first = (slot_flat[:, 0][None, :] == position).astype(jnp.float32)
    pick_second = (slot_flat[:, 1][None, :] == position).astype(jnp.float32)
    placing = (pick_first + pick_second).astype(jnp.bfloat16)
    dispatch = (
        jnp.dot(placing, normed.astype(jnp.bfloat16), preferred_element_type=jnp.float32)
        .astype(jnp.bfloat16)
        .reshape(experts, capacity, model_width)
    )
    arrived = lax.all_to_all(dispatch, "expert", split_axis=0, concat_axis=0, tiled=True)
    arrived_rows = arrived.reshape(slots_all, model_width)
    every_row = lax.all_gather(arrived_rows, "dp", axis=0, tiled=True)
    preact_first = jnp.dot(arrived_rows, first_weight, preferred_element_type=jnp.float32)
    active_first = jax.nn.gelu(preact_first, approximate=False).astype(jnp.bfloat16)
    result = lax.dot_general(
        active_first, second_weight, contract_last, preferred_element_type=jnp.float32
    ).astype(jnp.bfloat16)
    returned = lax.all_to_all(
        result.reshape(experts, capacity, model_width),
        "expert",
        split_axis=0,
        concat_axis=0,
        tiled=True,
    )
    picked = (
        jnp.take(
            returned.reshape(slots_all, model_width),
            slot_flat.reshape(-1),
            axis=0,
            mode="fill",
            fill_value=0,
        )
        .reshape(token_count, 2, model_width)
        .astype(jnp.float32)
    )
    block_out = middle_rows + jnp.sum(gate_values[:, :, None] * picked, axis=1)
    gate_grad = jnp.sum(picked * cot_float[:, None, :], axis=2)
    logit_step = gate_values[:, 0] * gate_values[:, 1] * (gate_grad[:, 0] - gate_grad[:, 1])
    columns = jnp.arange(experts, dtype=jnp.int32)[None, :]
    logit_grad = (
        (routes[:, 0:1] == columns).astype(jnp.float32)
        - (routes[:, 1:2] == columns).astype(jnp.float32)
    ) * logit_step[:, None]
    weighting = pick_first * gate_values[:, 0][None, :] + pick_second * gate_values[:, 1][None, :]
    sent_grad = (
        jnp.dot(weighting, cot_float, precision=highest)
        .astype(jnp.bfloat16)
        .reshape(experts, capacity, model_width)
    )
    again_grads = lax.all_to_all(sent_grad, "expert", split_axis=0, concat_axis=0, tiled=True)
    grad_rows = again_grads.reshape(slots_all, model_width)
    every_grad = lax.all_gather(grad_rows, "dp", axis=0, tiled=True)
    act_grad = jnp.dot(grad_rows, second_weight, preferred_element_type=jnp.float32)
    expert_pre_grad = (act_grad * gelu_slope(preact_first)).astype(jnp.bfloat16)
    row_grad = lax.dot_general(
        expert_pre_grad, first_weight, contract_last, preferred_element_type=jnp.float32
    ).astype(jnp.bfloat16)
    returned_grad = lax.all_to_all(
        row_grad.reshape(experts, capacity, model_width),
        "expert",
        split_axis=0,
        concat_axis=0,
        tiled=True,
    )
    gathered = (
        jnp.take(
            returned_grad.reshape(slots_all, model_width),
            slot_flat.reshape(-1),
            axis=0,
            mode="fill",
            fill_value=0,
        )
        .reshape(token_count, 2, model_width)
        .astype(jnp.float32)
    )
    normed_grad = jnp.sum(gathered, axis=1) + lax.dot_general(
        logit_grad, router, contract_last, precision=highest
    )
    router_local = lax.dot_general(normed, logit_grad, contract_first, precision=highest)
    middle_grad = input_grad(cot_float, normed_grad, scaled, inverse, ln_gains[1])
    middle_rounded = middle_grad.astype(jnp.bfloat16)
    mixed_grad = lax.dot_general(
        middle_rounded, full_out, contract_last, preferred_element_type=jnp.float32
    ).astype(jnp.bfloat16)
    scores_again = attention_scores(query_rows, key_rows, score_scale)
    probs_again = jnp.exp(scores_again - log_total).astype(jnp.bfloat16)
    grad_heads = mixed_grad.reshape(image_count, SEQ, HEADS, head_width)
    value_grad = jnp.einsum(
        "ihst,ishd->ithd", probs_again, grad_heads, preferred_element_type=jnp.float32
    )
    prob_grad = jnp.einsum(
        "ishd,ithd->ihst", grad_heads, value_rows, preferred_element_type=jnp.float32
    )
    prob_float = probs_again.astype(jnp.float32)
    row_delta = jnp.sum(prob_float * prob_grad, axis=3, keepdims=True)
    score_grad = (prob_float * (prob_grad - row_delta) * score_scale).astype(jnp.bfloat16)
    query_grad = jnp.einsum(
        "ihst,ithd->ishd", score_grad, key_rows, preferred_element_type=jnp.float32
    )
    key_grad = jnp.einsum(
        "ihst,ishd->ithd", score_grad, query_rows, preferred_element_type=jnp.float32
    )
    qkv_grad = (
        jnp.stack([query_grad, key_grad, value_grad], axis=2)
        .astype(jnp.bfloat16)
        .reshape(token_count, 3 * model_width)
    )
    attn_in_grad = lax.dot_general(
        qkv_grad, full_qkv, contract_last, preferred_element_type=jnp.float32
    )
    grad_tokens = input_grad(middle_grad, attn_in_grad, scaled_one, inverse_one, ln_gains[0])
    qkv_term = lax.dot_general(
        attn_in, qkv_grad, contract_first, preferred_element_type=jnp.float32
    )
    out_term = lax.dot_general(
        mixed_rows, middle_rounded, contract_first, preferred_element_type=jnp.float32
    )
    attention_share = lax.psum_scatter(
        jnp.concatenate([qkv_term, out_term], axis=1).astype(jnp.bfloat16),
        "expert",
        scatter_dimension=0,
        tiled=True,
    )
    norm_local = jnp.stack(
        [
            jnp.sum(attn_in_grad * scaled_one, axis=0),
            jnp.sum(normed_grad * scaled, axis=0),
            jnp.sum(attn_in_grad, axis=0),
            jnp.sum(normed_grad, axis=0),
        ]
    )
    attention_total = lax.psum(attention_share, "dp").astype(jnp.float32)
    small_parts = lax.all_gather(
        jnp.concatenate([router_local.T, norm_local], axis=0), ("dp", "expert"), axis=0
    )
    small_total = jnp.sum(small_parts, axis=0)
    grad_router = small_total[:experts].T
    grad_norm = small_total[experts:]
    grad_qkv = attention_total[:, : 3 * model_width]
    grad_out = attention_total[:, 3 * model_width :]
    moment_qkv = decay_rate * qkv_momentum + grad_qkv
    moment_out = decay_rate * out_momentum + grad_out
    whole_qkv = lax.all_gather(moment_qkv.astype(jnp.bfloat16), "expert", axis=0, tiled=True)
    whole_out = lax.all_gather(moment_out.astype(jnp.bfloat16), "expert", axis=0, tiled=True)
    row_base = lax.axis_index("dp") * dp_share
    every_moment = lax.all_gather(moment_pair, "dp", axis=0, tiled=True)
    every_preact = jnp.dot(every_row, first_weight, preferred_element_type=jnp.float32)
    every_active = jax.nn.gelu(every_preact, approximate=False).astype(jnp.bfloat16)
    every_act_grad = jnp.dot(every_grad, second_weight, preferred_element_type=jnp.float32)
    every_pre_grad = (every_act_grad * gelu_slope(every_preact)).astype(jnp.bfloat16)
    whole_first = lax.dot_general(
        every_row, every_pre_grad, contract_first, preferred_element_type=jnp.float32
    )
    whole_second = lax.dot_general(
        every_grad, every_active, contract_first, preferred_element_type=jnp.float32
    )
    grad_first = lax.dynamic_slice_in_dim(whole_first, row_base, dp_share, 0)
    grad_second = lax.dynamic_slice_in_dim(whole_second, row_base, dp_share, 0)
    moment_first = decay_rate * w_in_momentum[0] + grad_first
    moment_second = decay_rate * w_out_momentum[0] + grad_second
    iter_first = ortho_rows(
        decay_rate * every_moment[:, :hidden_units].astype(jnp.float32) + whole_first,
        row_base,
        dp_share,
    )
    iter_second = ortho_rows(
        decay_rate * every_moment[:, hidden_units:].astype(jnp.float32) + whole_second,
        row_base,
        dp_share,
    )
    expert_share = qkv_weight.shape[0]
    expert_base = lax.axis_index("expert") * expert_share
    iter_out = ortho_rows(whole_out.astype(jnp.float32), expert_base, expert_share)
    iter_qkv = ortho_rows(whole_qkv.astype(jnp.float32), expert_base, expert_share)
    new_norm_momentum = decay_rate * norm_momentum + grad_norm
    new_norm = jnp.concatenate([ln_gains, ln_biases], axis=0) - norm_rate * new_norm_momentum
    new_router_momentum = decay_rate * router_momentum + grad_router
    new_router = router - matrix_rate * ortho_tall(new_router_momentum).astype(jnp.float32)

    rows_first = lax.dynamic_slice_in_dim(first_weight, row_base, dp_share, 0).astype(jnp.float32)
    rows_second = lax.dynamic_slice_in_dim(second_weight, row_base, dp_share, 0).astype(jnp.float32)
    widen_factor = math.sqrt(max(1.0, hidden_units / model_width))
    new_first = rows_first - matrix_rate * widen_factor * iter_first.astype(jnp.float32)
    new_second = rows_second - matrix_rate * iter_second.astype(jnp.float32)
    new_qkv = qkv_weight.astype(jnp.float32) - matrix_rate * math.sqrt(3.0) * iter_qkv.astype(
        jnp.float32
    )
    new_out = out_weight.astype(jnp.float32) - matrix_rate * iter_out.astype(jnp.float32)
    return (
        block_out,
        grad_tokens,
        grad_norm,
        grad_router,
        grad_qkv,
        grad_out,
        grad_first[None],
        grad_second[None],
        new_norm,
        new_norm_momentum,
        new_router,
        new_router_momentum,
        new_qkv,
        moment_qkv,
        new_out,
        moment_out,
        new_first[None],
        moment_first[None],
        new_second[None],
        moment_second[None],
    )


def solution(mesh):
    in_specs = (
        P(("dp", "expert"), None),
        P(("dp", "expert"), None),
        P(("dp", "expert"), None),
        P(("dp", "expert"), None),
        P(),
        P(),
        P("expert", None),
        P("expert", None),
        P(),
        P("expert", None, None),
        P("expert", None, None),
        P(),
        P(),
        P("expert", None),
        P("expert", None),
        P("expert", "dp", None),
        P("expert", "dp", None),
    )
    out_specs = (
        P(("dp", "expert"), None),
        P(("dp", "expert"), None),
        P(),
        P(),
        P("expert", None),
        P("expert", None),
        P("expert", "dp", None),
        P("expert", "dp", None),
        P(),
        P(),
        P(),
        P(),
        P("expert", None),
        P("expert", None),
        P("expert", None),
        P("expert", None),
        P("expert", "dp", None),
        P("expert", "dp", None),
        P("expert", "dp", None),
        P("expert", "dp", None),
    )
    return jax.shard_map(body, mesh=mesh, in_specs=in_specs, out_specs=out_specs, check_vma=False)
```

```python
import math

import jax
import jax.numpy as jnp
from jax import lax
from jax.sharding import PartitionSpec as P

HEADS = 12
NS_STEPS = 5
SEQ = 197


quintic_one = 3.4445
quintic_two = -4.775
quintic_three = 2.0315
decay_rate = 0.9
matrix_rate = 0.2
norm_rate = 0.004
norm_eps = 1e-06
frob_eps = 1e-07
highest = lax.Precision.HIGHEST
contract_last = (((1,), (1,)), ((), ()))
contract_first = (((0,), (0,)), ((), ()))


def gelu_slope(preact):
    return (
        0.5 * (1.0 + lax.erf(preact * 0.7071067811865476))
        + preact * jnp.exp(-0.5 * preact * preact) * 0.3989422804014327
    )


def layer_stats(token_rows, gain, bias):
    centre = token_rows - jnp.mean(token_rows, axis=-1, keepdims=True)
    inverse = lax.rsqrt(jnp.mean(centre * centre, axis=-1, keepdims=True) + norm_eps)
    scaled = centre * inverse
    return (scaled, inverse, scaled * gain + bias)


def slot_index(choice_ids, order_rows, experts, capacity):
    token_count = choice_ids.shape[0]
    ranked = jnp.take(choice_ids, order_rows, axis=0)
    entries = jnp.concatenate([ranked[:, 0], ranked[:, 1]])
    onehot = (entries[:, None] == jnp.arange(experts, dtype=jnp.int32)[None, :]).astype(jnp.int32)
    before = jnp.cumsum(onehot, axis=0) - onehot
    ranked_slots = jnp.sum(before * onehot, axis=1).reshape(2, token_count).T
    slot_values = jnp.zeros((token_count, 2), jnp.int32).at[order_rows].set(ranked_slots)
    return jnp.where(
        slot_values < capacity, choice_ids * capacity + slot_values, experts * capacity
    )


def gates_of(logits, choice_ids):
    chosen = jnp.take_along_axis(logits, choice_ids, axis=1)
    first_gate = jax.nn.sigmoid(chosen[:, 0] - chosen[:, 1])
    return jnp.stack([first_gate, 1.0 - first_gate], axis=1)


def input_grad(base_grad, normed_grad, scaled, inverse, gain):
    lifted = normed_grad * gain
    centred = (
        lifted
        - jnp.mean(lifted, axis=-1, keepdims=True)
        - scaled * jnp.mean(lifted * scaled, axis=-1, keepdims=True)
    )
    return base_grad + inverse * centred


def ortho_tall(matrix):
    iterate = (matrix / (jnp.sqrt(jnp.sum(matrix * matrix)) + frob_eps)).astype(jnp.bfloat16)
    for iteration in range(NS_STEPS):
        gram_matrix = lax.dot_general(
            iterate, iterate, contract_first, preferred_element_type=jnp.float32
        ).astype(jnp.bfloat16)
        mixer_matrix = (
            quintic_two * gram_matrix.astype(jnp.float32)
            + quintic_three * jnp.dot(gram_matrix, gram_matrix, preferred_element_type=jnp.float32)
        ).astype(jnp.bfloat16)
        iterate = (
            quintic_one * iterate.astype(jnp.float32)
            + jnp.dot(iterate, mixer_matrix, preferred_element_type=jnp.float32)
        ).astype(jnp.bfloat16)
    return iterate


def ortho_rows(moment, row_start, row_count):
    norm = jnp.sqrt(jnp.sum(moment * moment)) + frob_eps
    iterate = (moment / norm).astype(jnp.bfloat16)
    for iteration in range(NS_STEPS):
        gram = lax.dot_general(
            iterate, iterate, contract_last, preferred_element_type=jnp.float32
        ).astype(jnp.bfloat16)
        gram_part, iter_part = gram, iterate
        if iteration == NS_STEPS - 1:
            gram_part = lax.dynamic_slice_in_dim(gram, row_start, row_count, 0)
            iter_part = lax.dynamic_slice_in_dim(iterate, row_start, row_count, 0)
        mixer = (
            quintic_two * gram_part.astype(jnp.float32)
            + quintic_three * jnp.dot(gram_part, gram, preferred_element_type=jnp.float32)
        ).astype(jnp.bfloat16)
        iterate = (
            quintic_one * iter_part.astype(jnp.float32)
            + jnp.dot(mixer, iterate, preferred_element_type=jnp.float32)
        ).astype(jnp.bfloat16)
    return iterate


def split_heads(qkv_rows, image_count, head_width):
    shaped = qkv_rows.reshape(image_count, SEQ, 3, HEADS, head_width)
    return (shaped[:, :, 0], shaped[:, :, 1], shaped[:, :, 2])


def attention_scores(query_rows, key_rows, score_scale):
    return (
        jnp.einsum("ishd,ithd->ihst", query_rows, key_rows, preferred_element_type=jnp.float32)
        * score_scale
    )


def body(
    tokens,
    cotangent,
    routes,
    priority,
    ln_gains,
    ln_biases,
    qkv_weight,
    out_weight,
    router,
    w_in,
    w_out,
    norm_momentum,
    router_momentum,
    qkv_momentum,
    out_momentum,
    w_in_momentum,
    w_out_momentum,
):
    token_count, model_width = tokens.shape
    experts = router.shape[1]
    hidden_units = w_in.shape[2]
    capacity = (token_count + experts - 1) // experts
    slots_all = experts * capacity
    dp_share = model_width // lax.axis_size("dp")
    image_count = token_count // SEQ
    head_width = model_width // HEADS
    score_scale = 1.0 / math.sqrt(head_width)
    first_weight = w_in[0]
    second_weight = w_out[0]
    cot_float = cotangent.astype(jnp.float32)
    full_qkv, full_out = (
        lax.all_gather(qkv_weight, "expert", axis=0, tiled=True),
        lax.all_gather(out_weight, "expert", axis=0, tiled=True),
    )
    moment_pair = jnp.concatenate(
        [w_in_momentum[0].astype(jnp.bfloat16), w_out_momentum[0].astype(jnp.bfloat16)], axis=1
    )
    every_moment = lax.all_gather(moment_pair, "dp", axis=0, tiled=True)
    token_float = tokens.astype(jnp.float32)
    scaled_one, inverse_one, normed_one = layer_stats(token_float, ln_gains[0], ln_biases[0])
    attn_in = normed_one.astype(jnp.bfloat16)
    qkv_rows = jnp.dot(attn_in, full_qkv, preferred_element_type=jnp.float32).astype(jnp.bfloat16)
    query_rows, key_rows, value_rows = split_heads(qkv_rows, image_count, head_width)
    scores = attention_scores(query_rows, key_rows, score_scale)
    log_total = jnp.log(jnp.sum(jnp.exp(scores), axis=3, keepdims=True))
    attn_probs = jnp.exp(scores - log_total).astype(jnp.bfloat16)
    mixed_rows = (
        jnp.einsum("ihst,ithd->ishd", attn_probs, value_rows, preferred_element_type=jnp.float32)
        .astype(jnp.bfloat16)
        .reshape(token_count, model_width)
    )
    middle_rows = token_float + jnp.dot(mixed_rows, full_out, preferred_element_type=jnp.float32)
    slot_flat = slot_index(routes, priority[0], experts, capacity)
    scaled, inverse, normed = layer_stats(middle_rows, ln_gains[1], ln_biases[1])
    logits = jnp.dot(normed, router, precision=highest)
    gate_values = gates_of(logits, routes)
    position = jnp.arange(slots_all, dtype=jnp.int32)[:, None]
    pick_first = (slot_flat[:, 0][None, :] == position).astype(jnp.float32)
    pick_second = (slot_flat[:, 1][None, :] == position).astype(jnp.float32)
    placing = (pick_first + pick_second).astype(jnp.bfloat16)
    dispatch = (
        jnp.dot(placing, normed.astype(jnp.bfloat16), preferred_element_type=jnp.float32)
        .astype(jnp.bfloat16)
        .reshape(experts, capacity, model_width)
    )
    arrived = lax.all_to_all(dispatch, "expert", split_axis=0, concat_axis=0, tiled=True)
    arrived_rows = arrived.reshape(slots_all, model_width)
    every_row = lax.all_gather(arrived_rows, "dp", axis=0, tiled=True)
    preact_first = jnp.dot(arrived_rows, first_weight, preferred_element_type=jnp.float32)
    active_first = jax.nn.gelu(preact_first, approximate=False).astype(jnp.bfloat16)
    result = lax.dot_general(
        active_first, second_weight, contract_last, preferred_element_type=jnp.float32
    ).astype(jnp.bfloat16)
    returned = lax.all_to_all(
        result.reshape(experts, capacity, model_width),
        "expert",
        split_axis=0,
        concat_axis=0,
        tiled=True,
    )
    picked = (
        jnp.take(
            returned.reshape(slots_all, model_width),
            slot_flat.reshape(-1),
            axis=0,
            mode="fill",
            fill_value=0,
        )
        .reshape(token_count, 2, model_width)
        .astype(jnp.float32)
    )
    block_out = middle_rows + jnp.sum(gate_values[:, :, None] * picked, axis=1)
    gate_grad = jnp.sum(picked * cot_float[:, None, :], axis=2)
    logit_step = gate_values[:, 0] * gate_values[:, 1] * (gate_grad[:, 0] - gate_grad[:, 1])
    columns = jnp.arange(experts, dtype=jnp.int32)[None, :]
    logit_grad = (
        (routes[:, 0:1] == columns).astype(jnp.float32)
        - (routes[:, 1:2] == columns).astype(jnp.float32)
    ) * logit_step[:, None]
    weighting = pick_first * gate_values[:, 0][None, :] + pick_second * gate_values[:, 1][None, :]
    sent_grad = (
        jnp.dot(weighting, cot_float, precision=highest)
        .astype(jnp.bfloat16)
        .reshape(experts, capacity, model_width)
    )
    again_grads = lax.all_to_all(sent_grad, "expert", split_axis=0, concat_axis=0, tiled=True)
    grad_rows = again_grads.reshape(slots_all, model_width)
    every_grad = lax.all_gather(grad_rows, "dp", axis=0, tiled=True)
    act_grad = jnp.dot(grad_rows, second_weight, preferred_element_type=jnp.float32)
    expert_pre_grad = (act_grad * gelu_slope(preact_first)).astype(jnp.bfloat16)
    row_grad = lax.dot_general(
        expert_pre_grad, first_weight, contract_last, preferred_element_type=jnp.float32
    ).astype(jnp.bfloat16)
    returned_grad = lax.all_to_all(
        row_grad.reshape(experts, capacity, model_width),
        "expert",
        split_axis=0,
        concat_axis=0,
        tiled=True,
    )
    gathered = (
        jnp.take(
            returned_grad.reshape(slots_all, model_width),
            slot_flat.reshape(-1),
            axis=0,
            mode="fill",
            fill_value=0,
        )
        .reshape(token_count, 2, model_width)
        .astype(jnp.float32)
    )
    normed_grad = jnp.sum(gathered, axis=1) + lax.dot_general(
        logit_grad, router, contract_last, precision=highest
    )
    router_local = lax.dot_general(normed, logit_grad, contract_first, precision=highest)
    middle_grad = input_grad(cot_float, normed_grad, scaled, inverse, ln_gains[1])
    middle_grad, every_moment = lax.optimization_barrier((middle_grad, every_moment))
    middle_rounded = middle_grad.astype(jnp.bfloat16)
    mixed_grad = lax.dot_general(
        middle_rounded, full_out, contract_last, preferred_element_type=jnp.float32
    ).astype(jnp.bfloat16)
    scores_again = attention_scores(query_rows, key_rows, score_scale)
    probs_again = jnp.exp(scores_again - log_total).astype(jnp.bfloat16)
    grad_heads = mixed_grad.reshape(image_count, SEQ, HEADS, head_width)
    value_grad = jnp.einsum(
        "ihst,ishd->ithd", probs_again, grad_heads, preferred_element_type=jnp.float32
    )
    prob_grad = jnp.einsum(
        "ishd,ithd->ihst", grad_heads, value_rows, preferred_element_type=jnp.float32
    )
    prob_float = probs_again.astype(jnp.float32)
    row_delta = jnp.sum(prob_float * prob_grad, axis=3, keepdims=True)
    score_grad = (prob_float * (prob_grad - row_delta) * score_scale).astype(jnp.bfloat16)
    query_grad = jnp.einsum(
        "ihst,ithd->ishd", score_grad, key_rows, preferred_element_type=jnp.float32
    )
    key_grad = jnp.einsum(
        "ihst,ishd->ithd", score_grad, query_rows, preferred_element_type=jnp.float32
    )
    qkv_grad = (
        jnp.stack([query_grad, key_grad, value_grad], axis=2)
        .astype(jnp.bfloat16)
        .reshape(token_count, 3 * model_width)
    )
    qkv_grad, every_row, every_grad = lax.optimization_barrier((qkv_grad, every_row, every_grad))
    attn_in_grad = lax.dot_general(
        qkv_grad, full_qkv, contract_last, preferred_element_type=jnp.float32
    )
    grad_tokens = input_grad(middle_grad, attn_in_grad, scaled_one, inverse_one, ln_gains[0])
    qkv_term = lax.dot_general(
        attn_in, qkv_grad, contract_first, preferred_element_type=jnp.float32
    )
    out_term = lax.dot_general(
        mixed_rows, middle_rounded, contract_first, preferred_element_type=jnp.float32
    )
    attention_share = lax.psum_scatter(
        jnp.concatenate([qkv_term, out_term], axis=1).astype(jnp.bfloat16),
        "expert",
        scatter_dimension=0,
        tiled=True,
    )
    norm_local = jnp.stack(
        [
            jnp.sum(attn_in_grad * scaled_one, axis=0),
            jnp.sum(normed_grad * scaled, axis=0),
            jnp.sum(attn_in_grad, axis=0),
            jnp.sum(normed_grad, axis=0),
        ]
    )
    attention_total = lax.psum(attention_share, "dp").astype(jnp.float32)
    small_parts = lax.all_gather(
        jnp.concatenate([router_local.T, norm_local], axis=0), ("dp", "expert"), axis=0
    )
    small_total = jnp.sum(small_parts, axis=0)
    grad_router = small_total[:experts].T
    grad_norm = small_total[experts:]
    grad_qkv = attention_total[:, : 3 * model_width]
    grad_out = attention_total[:, 3 * model_width :]
    moment_qkv = decay_rate * qkv_momentum + grad_qkv
    moment_out = decay_rate * out_momentum + grad_out
    whole_qkv = lax.all_gather(moment_qkv.astype(jnp.bfloat16), "expert", axis=0, tiled=True)
    whole_out = lax.all_gather(moment_out.astype(jnp.bfloat16), "expert", axis=0, tiled=True)
    row_base = lax.axis_index("dp") * dp_share
    every_preact = jnp.dot(every_row, first_weight, preferred_element_type=jnp.float32)
    every_active = jax.nn.gelu(every_preact, approximate=False).astype(jnp.bfloat16)
    every_act_grad = jnp.dot(every_grad, second_weight, preferred_element_type=jnp.float32)
    every_pre_grad = (every_act_grad * gelu_slope(every_preact)).astype(jnp.bfloat16)
    dp_count = lax.axis_size("dp")
    dp_half = dp_count // 2
    role = lax.axis_index("dp") // dp_half
    pair_index = lax.axis_index("dp") % dp_half
    does_first = role == 0
    role_left = jnp.where(does_first, every_row, every_grad)
    role_right = jnp.where(does_first, every_pre_grad, every_active)
    role_moment = jnp.where(
        does_first, every_moment[:, :hidden_units], every_moment[:, hidden_units:]
    )
    role_grad = lax.dot_general(
        role_left, role_right, contract_first, preferred_element_type=jnp.float32
    )
    role_iter = ortho_rows(
        decay_rate * role_moment.astype(jnp.float32) + role_grad,
        pair_index * (2 * dp_share),
        2 * dp_share,
    )
    near_rows = lax.ppermute(
        lax.dynamic_slice_in_dim(role_iter, role * dp_share, dp_share, 0),
        "dp",
        [(r * dp_half + k, 2 * k + r) for r in range(2) for k in range(dp_half)],
    )
    far_rows = lax.ppermute(
        lax.dynamic_slice_in_dim(role_iter, (1 - role) * dp_share, dp_share, 0),
        "dp",
        [(r * dp_half + k, 2 * k + 1 - r) for r in range(2) for k in range(dp_half)],
    )
    is_even = lax.axis_index("dp") % 2 == 0
    iter_first = jnp.where(is_even, near_rows, far_rows)
    iter_second = jnp.where(is_even, far_rows, near_rows)
    grad_first = lax.dot_general(
        lax.dynamic_slice_in_dim(every_row, row_base, dp_share, 1),
        every_pre_grad,
        contract_first,
        preferred_element_type=jnp.float32,
    )
    grad_second = lax.dot_general(
        lax.dynamic_slice_in_dim(every_grad, row_base, dp_share, 1),
        every_active,
        contract_first,
        preferred_element_type=jnp.float32,
    )
    moment_first = decay_rate * w_in_momentum[0] + grad_first
    moment_second = decay_rate * w_out_momentum[0] + grad_second
    expert_share = qkv_weight.shape[0]
    expert_base = lax.axis_index("expert") * expert_share
    iter_out = ortho_rows(whole_out.astype(jnp.float32), expert_base, expert_share)
    iter_qkv = ortho_rows(whole_qkv.astype(jnp.float32), expert_base, expert_share)
    new_norm_momentum = decay_rate * norm_momentum + grad_norm
    new_norm = jnp.concatenate([ln_gains, ln_biases], axis=0) - norm_rate * new_norm_momentum
    new_router_momentum = decay_rate * router_momentum + grad_router
    new_router = router - matrix_rate * ortho_tall(new_router_momentum).astype(jnp.float32)

    rows_first = lax.dynamic_slice_in_dim(first_weight, row_base, dp_share, 0).astype(jnp.float32)
    rows_second = lax.dynamic_slice_in_dim(second_weight, row_base, dp_share, 0).astype(jnp.float32)
    widen_factor = math.sqrt(max(1.0, hidden_units / model_width))
    new_first = rows_first - matrix_rate * widen_factor * iter_first.astype(jnp.float32)
    new_second = rows_second - matrix_rate * iter_second.astype(jnp.float32)
    new_qkv = qkv_weight.astype(jnp.float32) - matrix_rate * math.sqrt(3.0) * iter_qkv.astype(
        jnp.float32
    )
    new_out = out_weight.astype(jnp.float32) - matrix_rate * iter_out.astype(jnp.float32)
    return (
        block_out,
        grad_tokens,
        grad_norm,
        grad_router,
        grad_qkv,
        grad_out,
        grad_first[None],
        grad_second[None],
        new_norm,
        new_norm_momentum,
        new_router,
        new_router_momentum,
        new_qkv,
        moment_qkv,
        new_out,
        moment_out,
        new_first[None],
        moment_first[None],
        new_second[None],
        moment_second[None],
    )


def solution(mesh):
    in_specs = (
        P(("dp", "expert"), None),
        P(("dp", "expert"), None),
        P(("dp", "expert"), None),
        P(("dp", "expert"), None),
        P(),
        P(),
        P("expert", None),
        P("expert", None),
        P(),
        P("expert", None, None),
        P("expert", None, None),
        P(),
        P(),
        P("expert", None),
        P("expert", None),
        P("expert", "dp", None),
        P("expert", "dp", None),
    )
    out_specs = (
        P(("dp", "expert"), None),
        P(("dp", "expert"), None),
        P(),
        P(),
        P("expert", None),
        P("expert", None),
        P("expert", "dp", None),
        P("expert", "dp", None),
        P(),
        P(),
        P(),
        P(),
        P("expert", None),
        P("expert", None),
        P("expert", None),
        P("expert", None),
        P("expert", "dp", None),
        P("expert", "dp", None),
        P("expert", "dp", None),
        P("expert", "dp", None),
    )
    return jax.shard_map(body, mesh=mesh, in_specs=in_specs, out_specs=out_specs, check_vma=False)
```
